32 devices in a mesh: strip: 4 (over z), date: 8 (over y, x, core).
Axes of the slice: x: 2, y: 2, z: 4, core: 2. Of those that a mesh axis runs over, the one named last changes fastest.
Arguments:
- images: bfloat16 [128, 256, 128], P('date', 'strip'), may hold values from 0.19921875 to 5
- inverse_blocks: float32 [2, 8, 128, 128], P(None, 'strip', 'date'), as said below
- pair_first: int32 [256], P('date'), may hold values from 0 to 15
- pair_block: int32 [256, 1], P('date'), may hold values from 0 to 7; in each aligned block of 32 rows (0 to 31, 32 to 63, ...) at most 8 rows name the same one
- pair_second: int32 [256], P('date'), may hold values from 0 to 15
- pair_count: int32 [8], P('date'), may hold values from 8 to 32, as said below
- shifts: int32 [256, 2, 8], P('date', None, 'strip'), may hold values from -8 to 8
- anchors: int32 [8], P('strip'), may hold values from 0 to 96, as said below
Outputs:
- pair_offsets: float32 [256, 2, 8], P('date', None, 'strip')
- series: float32 [2, 8, 128], P(None, 'strip', 'date')
The draws below stay inside these ranges and needn't reach their ends.
Inputs may be any that keep to these rules, and one draw needn't show every extreme that they name: `pair_block`: among the 32 slots of one date block at most 8 name one partner block, and some block is named that often. `pair_count`: slots 0 to count - 1 of a date block are live; slots at or past the count carry no pair, and their partner windows need not be sent. One block has all 32 live, one has 8, every other block 24 or more. `anchors`: chip q starts at column (q % 2) * 64 plus 0 to 32. `inverse_blocks`: symmetric in its last two dimensions.
All inputs are finite; a program needn't handle non-finite values.
Results may differ from the reference program's by a relative error of at most 0.008.
Values may be sent and summed in bfloat16 or wider, within the bound.
A program may use at most 64 MiB of HBM per device.

```python
import math
import jax
import jax.numpy as jnp
import numpy as np
from jax import lax

CHIP = 64
SMAX = 8
DATE_DEV = 16
NCHIP = 2
PAIR_DEV = 32
CAP = 8
BLOCKS = 8
NDATE = 128
PAIRS = 256
COLS = 128
BAND_ROWS = 256
CHIPS_ALL = 8


def draw_inverse_blocks(key, part):
    subkeys = jax.random.split(key, 2)
    noise_part = jax.random.normal(subkeys[0], (2, CHIPS_ALL, NDATE, NDATE), jnp.float32) * (0.5 / math.sqrt(NDATE))
    mirror = (noise_part + jnp.swapaxes(noise_part, 2, 3)) * (1.0 / math.sqrt(2.0))
    diag_vals = jnp.exp(jax.random.uniform(subkeys[1], (2, CHIPS_ALL, NDATE), jnp.float32, math.log(0.5), math.log(2.0)))
    result = mirror + diag_vals[..., None] * jnp.eye(NDATE, dtype=jnp.float32)
    return result


def draw_pair_count(key, part):
    subkeys = jax.random.split(key, 2)
    counts = jax.random.randint(subkeys[0], (BLOCKS,), 3 * PAIR_DEV // 4, PAIR_DEV + 1, jnp.int32)
    shuffled = jax.random.permutation(subkeys[1], BLOCKS)
    counts = counts.at[shuffled[0]].set(PAIR_DEV)
    counts = counts.at[shuffled[1]].set(PAIR_DEV // 4)
    return counts


def draw_anchors(key, part):
    chip_ids = jnp.arange(CHIPS_ALL, dtype=jnp.int32)
    offsets_in = jax.random.randint(key, (CHIPS_ALL,), 0, CHIP // 2 + 1, jnp.int32)
    offsets_in = offsets_in.at[0].set(0)
    offsets_in = offsets_in.at[CHIPS_ALL - 1].set(CHIP // 2)
    return chip_ids % NCHIP * CHIP + offsets_in


def touch_ends(entries, rng, least, largest):
    extent = entries.shape
    place = [jax.random.randint(jax.random.fold_in(rng, axis), (), 0, extent[axis]) for axis in range(len(extent))]
    entries = entries.at[tuple(place)].set(least)
    longest = extent.index(max(extent))
    place[longest] = (place[longest] + 1) % extent[longest]
    return entries.at[tuple(place)].set(largest)


def shard_levels(own_key, shape, pieces, low, top_value):
    loudness, own = 1.0, jax.random.fold_in(own_key, 6)
    for axis_at, shards_of in pieces:
        heights = jnp.exp(jax.random.uniform(jax.random.fold_in(own, axis_at), (shards_of,), jnp.float32, low / len(pieces), top_value / len(pieces)))
        loudness = loudness * jnp.repeat(heights, shape[axis_at] // shards_of).reshape([-1 if axis == axis_at else 1 for axis in range(len(shape))])
    return loudness


def routed_block(stream_key, own, number, rows, amount, top, limit, lean):
    sequence = jax.random.permutation(stream_key, amount)
    packed, usual = shares(amount, rows * top, limit, lean, True), shares(amount, rows * top, limit, lean, False)
    places = jnp.arange(amount)

    def named(tallies, turn):
        used = int((tallies > 0).sum())
        fixed = max(1, used // 4)
        moved = fixed + (places - fixed + turn * (used - fixed)) % max(1, amount - fixed)
        return jnp.zeros((amount,), jnp.int32).at[sequence[jnp.where(places < fixed, places, moved)]].set(jnp.asarray(tallies, jnp.int32))

    tallies = jnp.where(number % 4 == 0, named(packed, number // 4), named(usual, number - number // 4 - 1))
    mixed = jax.random.permutation(jax.random.fold_in(own, 3), amount)
    giver, sink = mixed[0:amount // 2 * 2:2], mixed[1:amount // 2 * 2:2]
    room = jnp.minimum(tallies[giver] - 1, limit - tallies[sink]) // 2
    room = jnp.where((giver == sequence[0]) | (sink == sequence[0]) | (tallies[sink] == 0), 0, jnp.maximum(room, 0))
    moved = jax.random.randint(jax.random.fold_in(own, 4), (amount // 2,), 0, 1 << 20) % (room + 1)
    tallies = tallies.at[giver].add(-moved).at[sink].add(moved)
    items = jnp.searchsorted(jnp.cumsum(tallies), jnp.arange(rows * top), side="right").astype(jnp.int32)
    grid = items.reshape(top, rows).T
    grid = grid[jax.random.permutation(jax.random.fold_in(own, 1), rows)]
    turn = jax.random.randint(jax.random.fold_in(own, 2), (rows, 1), 0, top)
    return jnp.take_along_axis(grid, (jnp.arange(top)[None, :] + turn) % top, axis=1)


def shares(count, total, limit, lean, full):
    portions = [(1 << 20) // math.isqrt(grade ** lean) + 1 for grade in range(1, count + 1)]
    largest = limit if full else min(limit, max(-(-total // count), total * portions[0] // sum(portions)))
    least = 1 if total - largest >= count - 1 else 0
    given, rest = [largest] + [least] * (count - 1), total - largest - least * (count - 1)
    while rest > 0:
        free = [i for i in range(1, count) if given[i] < largest] or [i for i in range(1, count) if given[i] < limit]
        pool, left = sum([portions[i] for i in free]), rest
        for i in free:
            extra = min(limit - given[i], max(1, left * portions[i] // pool), rest)
            given[i] = given[i] + extra
            rest = rest - extra
    return np.array(given)


def setup_inputs(seed: int = 0) -> dict:
    streams_of = jax.random.split(jax.random.key(seed), 9)
    images = jnp.clip(jnp.exp(math.log(5.0) - 3.2227897 * jax.random.uniform(streams_of[0], (NDATE, BAND_ROWS, COLS), jnp.float32) ** shard_levels(streams_of[0], (NDATE, BAND_ROWS, COLS), ((0, 8), (1, 4)), -0.2, 0.2)), 0.19921875, 5.0).astype(jnp.bfloat16)
    inverse_blocks = draw_inverse_blocks(jax.random.fold_in(streams_of[8], 71), 0)
    pair_first = touch_ends(jax.random.randint(streams_of[2], (PAIRS,), 0, DATE_DEV), jax.random.fold_in(streams_of[2], 1), 0, DATE_DEV - 1).astype(jnp.int32)
    pair_block_keys = jax.random.split(jax.random.fold_in(streams_of[3], 1), PAIRS // PAIR_DEV)
    pair_block_turns = jax.random.permutation(jax.random.fold_in(streams_of[3], 3), PAIRS // PAIR_DEV)
    pair_block = jax.vmap(lambda own, number: routed_block(jax.random.fold_in(streams_of[3], 2), own, number, PAIR_DEV, BLOCKS, 1, CAP, 1))(pair_block_keys, pair_block_turns).reshape((PAIRS, 1))
    pair_second = touch_ends(jax.random.randint(streams_of[4], (PAIRS,), 0, DATE_DEV), jax.random.fold_in(streams_of[4], 1), 0, DATE_DEV - 1).astype(jnp.int32)
    pair_count = draw_pair_count(jax.random.fold_in(streams_of[8], 71), 0)
    shifts = touch_ends(jax.random.randint(streams_of[6], (PAIRS, 2, CHIPS_ALL), -SMAX, SMAX + 1), jax.random.fold_in(streams_of[6], 1), -SMAX, SMAX).astype(jnp.int32)
    anchors = draw_anchors(jax.random.fold_in(streams_of[8], 71), 0)
    return {"images": images, "inverse_blocks": inverse_blocks, "pair_first": pair_first, "pair_block": pair_block, "pair_second": pair_second, "pair_count": pair_count, "shifts": shifts, "anchors": anchors}


def make_tables(length):
    counter = jnp.arange(length, dtype=jnp.int32)
    products = (counter[:, None] * counter[None, :]) % length
    radians = products.astype(jnp.float32) * (2.0 * math.pi / length)
    cosine = jnp.cos(radians)
    sine_part = -jnp.sin(radians)
    forward = jnp.concatenate([cosine, sine_part], axis=1).astype(jnp.bfloat16)
    over_len = 2 * length
    signed = jnp.where(counter < length // 2, counter, counter - length)
    places = jnp.arange(over_len, dtype=jnp.int32)
    turned = (signed[:, None] * places[None, :]) % over_len
    angles = turned.astype(jnp.float32) * (2.0 * math.pi / over_len)
    vcosine = jnp.cos(angles)
    vsine = jnp.sin(angles)
    top_rows = jnp.concatenate([vcosine, vsine], axis=1)
    low_rows = jnp.concatenate([-vsine, vcosine], axis=1)
    inverse_rows = jnp.concatenate([top_rows, low_rows], axis=0).astype(jnp.bfloat16)
    displace = (((places + length) % over_len) - length).astype(jnp.float32) * 0.5
    return (forward, cosine.astype(jnp.bfloat16), sine_part.astype(jnp.bfloat16), inverse_rows,
            vcosine.T.astype(jnp.bfloat16), vsine.T.astype(jnp.bfloat16), displace)


def product(form, left, right):
    return jnp.einsum(form, left.astype(jnp.float32), right.astype(jnp.float32), precision=lax.Precision.HIGHEST)


def spectra(windows, tables):
    forward, cosine_b, sine_b = tables[0], tables[1], tables[2]
    length = windows.shape[-1]
    values = windows.astype(jnp.float32)
    centred = (values - jnp.mean(values, axis=(1, 2), keepdims=True)).astype(jnp.bfloat16)
    section_one = product("bmn,nk->bmk", centred, forward).astype(jnp.bfloat16)
    with_cos = product("km,bmj->bkj", cosine_b, section_one)
    with_sin = product("km,bmj->bkj", sine_b, section_one)
    real_part = with_cos[:, :, :length] - with_sin[:, :, length:]
    imag_part = with_sin[:, :, :length] + with_cos[:, :, length:]
    return jnp.concatenate([real_part, imag_part], axis=2).astype(jnp.bfloat16)


def centroid(near_spec, far_spec, tables):
    inverse_rows, back_cos, back_sin, displace = tables[3], tables[4], tables[5], tables[6]
    length = near_spec.shape[-1] // 2
    near_re = near_spec[:, :, :length].astype(jnp.float32)
    near_im = near_spec[:, :, length:].astype(jnp.float32)
    far_re = far_spec[:, :, :length].astype(jnp.float32)
    far_im = far_spec[:, :, length:].astype(jnp.float32)
    cross_re = near_re * far_re + near_im * far_im
    cross_im = near_im * far_re - near_re * far_im
    cross_spec = jnp.concatenate([cross_re, cross_im], axis=2).astype(jnp.bfloat16)
    along = product("bun,nl->bul", cross_spec, inverse_rows).astype(jnp.bfloat16)
    half_width = along.shape[-1] // 2
    surface = product("ku,bul->bkl", back_cos, along[:, :, :half_width]) - product("ku,bul->bkl", back_sin, along[:, :, half_width:])
    energy = surface * surface
    norm_val = jnp.mean(energy, axis=(1, 2)) + 1e-6
    row_shift = jnp.mean(energy * displace[None, :, None], axis=(1, 2)) / norm_val
    col_shift = jnp.mean(energy * displace[None, None, :], axis=(1, 2)) / norm_val
    return jnp.stack([row_shift, col_shift], axis=1)


def reference(images, inverse_blocks, pair_first, pair_block, pair_second, pair_count, shifts, anchors):
    length = CHIP
    margin = SMAX
    tables = make_tables(length)
    padded = jnp.pad(images, ((0, 0), (margin, margin), (margin, margin + length // 2)))
    chip_ids = jnp.arange(CHIPS_ALL, dtype=jnp.int32)
    row_base = ((chip_ids // NCHIP) * length + margin).astype(jnp.int32)
    col_base = (anchors + margin).astype(jnp.int32)

    def cut_window(image_rows, row_at, col_at):
        return lax.dynamic_slice(image_rows, (row_at, col_at), (length, length))

    def one_pair(slot):
        block_id = slot // PAIR_DEV
        first_id = (block_id * DATE_DEV + pair_first[slot]).astype(jnp.int32)
        second_id = (pair_block[slot, 0] * DATE_DEV + pair_second[slot]).astype(jnp.int32)
        live_mask = ((slot % PAIR_DEV) < pair_count[block_id]).astype(jnp.float32)
        near_img = lax.dynamic_index_in_dim(padded, first_id, 0, keepdims=False)
        far_img = lax.dynamic_index_in_dim(padded, second_id, 0, keepdims=False)
        near_win = jax.vmap(cut_window, in_axes=(None, 0, 0))(near_img, row_base, col_base)
        far_win = jax.vmap(cut_window, in_axes=(None, 0, 0))(far_img, (row_base + shifts[slot, 0]).astype(jnp.int32), (col_base + shifts[slot, 1]).astype(jnp.int32))
        found = centroid(spectra(near_win, tables), spectra(far_win, tables), tables)
        return (shifts[slot].astype(jnp.float32) + found.T) * live_mask

    pair_offsets = lax.map(one_pair, jnp.arange(PAIRS, dtype=jnp.int32))
    slot_ids = jnp.arange(PAIRS, dtype=jnp.int32)
    first_all = ((slot_ids // PAIR_DEV) * DATE_DEV + pair_first).astype(jnp.int32)
    second_all = (pair_block[:, 0] * DATE_DEV + pair_second).astype(jnp.int32)
    rhs_all = jax.ops.segment_sum(pair_offsets, second_all, num_segments=NDATE) - jax.ops.segment_sum(pair_offsets, first_all, num_segments=NDATE)
    rhs_all = jnp.transpose(rhs_all, (1, 2, 0))
    series = jnp.einsum("xqde,xqe->xqd", inverse_blocks, rhs_all, precision=lax.Precision.HIGHEST)
    return (pair_offsets, series)
```

```python
import functools
import math

import jax
import jax.numpy as jnp
import numpy as np
from jax import lax
from jax.experimental import pallas as pl
from jax.experimental.pallas import tpu as pltpu
from jax.sharding import PartitionSpec as P

SMAX = 8
MESH = pl.DeviceIdType.MESH
F32, BF16 = jnp.float32, jnp.bfloat16


def make_tables(length):
    counter = np.arange(length)
    radians = (counter[:, None] * counter[None, :] % length) * (2.0 * math.pi / length)
    cosine, sine = np.cos(radians), -np.sin(radians)
    over = 2 * length
    signed = np.where(counter < length // 2, counter, counter - length)
    places = np.arange(over)
    angles = (signed[:, None] * places[None, :] % over) * (2.0 * math.pi / over)
    vcos, vsin = np.cos(angles), np.sin(angles)
    forward = np.concatenate([cosine, sine, -sine, cosine], axis=1)
    forward = np.concatenate([forward, np.zeros_like(forward)], axis=0)
    rows = np.concatenate([cosine, sine], axis=1)
    one = np.concatenate([vcos, vsin], axis=1)
    two = np.concatenate([-vsin, vcos], axis=1)
    back = np.concatenate([one, one, two, -two], axis=0)
    final = np.concatenate([vcos.T, -vsin.T], axis=1)
    return [jnp.asarray(t.astype(np.float32)).astype(BF16) for t in (forward, rows, back, final)]


def gather_kernel(n, strips, img, top, bot, grid_out, halo_out, local, send, recv):
    me = lax.axis_index("date")
    strip = lax.axis_index("strip")
    up, down = lax.rem(strip + strips - 1, strips), lax.rem(strip + 1, strips)
    half = img.shape[0] // 2
    first, second = pl.ds(0, half), pl.ds(half, img.shape[0] - half)

    def sent(k, src, dst, where):
        return pltpu.make_async_remote_copy(
            src_ref=src,
            dst_ref=dst,
            send_sem=send.at[k],
            recv_sem=recv.at[k],
            device_id=where,
            device_id_type=MESH,
        )

    hier = n == 8
    if hier:
        steps = [1, 2, 4]
        peers = [jnp.bitwise_xor(me, j) for j in steps]
    else:
        peers = [lax.rem(me + j, n) for j in range(1, n)]
    barrier = pltpu.get_barrier_semaphore()
    for peer in peers:
        pl.semaphore_signal(barrier, inc=1, device_id={"date": peer}, device_id_type=MESH)
    for other in (up, down):
        pl.semaphore_signal(barrier, inc=1, device_id={"strip": other}, device_id_type=MESH)
    own = pltpu.make_async_copy(img, grid_out.at[me], local.at[0])
    own.start()
    pl.semaphore_wait(barrier, len(peers) + 2)

    z_up = sent(0, top, halo_out.at[me, 0], {"strip": up})
    z_down = sent(1, bot, halo_out.at[me, 1], {"strip": down})
    if not hier:
        z_up.start()
        z_down.start()
        mains = []
        for j, peer in enumerate(peers):
            mains.append(sent(2 + j, img, grid_out.at[me], {"date": peer}))
            mains[-1].start()
        z_up.wait()
        z_down.wait()
        for j, peer in enumerate(peers):
            mains.append(sent(n + 1 + j, halo_out.at[me], halo_out.at[me], {"date": peer}))
            mains[-1].start()
        for copy in mains:
            copy.wait()
        own.wait()
        return

    core, ex, wy = ({"date": peer} for peer in peers)

    def family(base, own_ref, out, one, two):
        def made(k, block, part, where, mine=False):
            src = own_ref.at[part] if mine else out.at[block, part]
            return sent(base + k, src, out.at[block, part], where)

        near_x, near_y, diag = (jnp.bitwise_xor(me, j) for j in (2, 4, 6))
        return [
            made(0, me, one, wy, True),
            made(1, me, two, wy, True),
            made(2, me, two, ex, True),
            made(3, me, one, ex, True),
            made(4, me, one, core, True),
            made(5, near_y, one, ex),
            made(6, near_y, one, core),
            made(7, near_x, two, wy),
            made(8, near_x, two, core),
            made(9, near_y, two, core),
            made(10, near_x, one, core),
            made(11, diag, one, core),
            made(12, diag, two, core),
            made(13, me, two, core, True),
        ]

    main = family(2, img, grid_out, first, second)
    halo = family(16, halo_out.at[me], halo_out, 0, 1)

    def run(copies, ids):
        for k in ids:
            copies[k].start()

    run(main, (0, 2))
    z_up.start()
    z_down.start()
    run(main, (1, 3, 4, 13))
    main[0].wait_recv()
    run(main, (5, 6))
    main[2].wait_recv()
    run(main, (7, 8))
    z_up.wait_recv()
    z_down.wait_recv()
    run(halo, (0, 2, 1, 3, 4, 13))
    main[1].wait_recv()
    run(main, (9,))
    main[3].wait_recv()
    run(main, (10,))
    main[5].wait_recv()
    run(main, (11,))
    main[7].wait_recv()
    run(main, (12,))
    halo[0].wait_recv()
    run(halo, (5, 6))
    halo[2].wait_recv()
    run(halo, (7, 8))
    halo[1].wait_recv()
    run(halo, (9,))
    halo[3].wait_recv()
    run(halo, (10,))
    halo[5].wait_recv()
    run(halo, (11,))
    halo[7].wait_recv()
    run(halo, (12,))
    for k in (4, 13, 6, 8, 9, 10, 11, 12):
        main[k].wait_recv()
        halo[k].wait_recv()
    for copy in main + halo + [z_up, z_down]:
        copy.wait_send()
    own.wait()


def pairs_kernel(
    n, strips, batch,
    first_s, block_s, second_s, count_s, shifts_s, anchors_s,
    img, grid_in, halo_in, forward, rows, back, final,
    offsets_out, partial_out,
    wide, far, near, spec, sums, moments, moves,
):
    dates, length, cols = img.shape
    pairs, chips = first_s.shape[0], anchors_s.shape[0]
    me, strip = lax.axis_index("date"), lax.axis_index("strip")
    lane = lax.broadcasted_iota(jnp.int32, (length, cols), 1)
    has_up, has_down = strip > 0, strip < strips - 1
    half_dates = dates // 2

    def turned(value, start):
        rolled = pltpu.roll(value, lax.rem(2 * cols - start, cols), 1)
        inside = (lane >= -start) & (lane < cols - start)
        return jnp.where(inside, rolled, 0.0).astype(BF16)

    def near_cut(d, carry):
        value = img[d].astype(F32)
        for c in range(chips):
            near[d * chips + c] = turned(value, anchors_s[c])
        return carry

    lax.fori_loop(0, dates, near_cut, 0, unroll=4)

    def far_cut(p, carry):
        block, day = block_s[p], second_s[p]
        wide[p, pl.ds(SMAX, length)] = grid_in[block * dates + day].astype(F32)
        odd = lax.rem(day, 2) == 1
        tile = block * dates + day // 2
        for side, at, has in ((0, SMAX + length, has_down), (1, 0, has_up)):
            held = halo_in[tile + side * half_dates].astype(F32)
            edge = jnp.where(odd, held[SMAX:], held[:SMAX])
            wide[p, pl.ds(at, SMAX)] = jnp.where(has, edge, 0.0)
        for c in range(chips):
            value = wide[p, pl.ds(SMAX + shifts_s[0, c, p], length)]
            far[p * chips + c] = turned(value, anchors_s[c] + shifts_s[1, c, p])
        place = lax.broadcasted_iota(jnp.int32, (1, cols), 1)
        row = jnp.zeros((1, cols), F32)
        for x in range(2):
            for c in range(chips):
                row = jnp.where(place == x * chips + c, shifts_s[x, c, p].astype(F32), row)
        row = jnp.where(place == 2 * chips, (block * dates + day).astype(F32), row)
        row = jnp.where(place == 2 * chips + 1, (me * dates + first_s[p]).astype(F32), row)
        moves[pl.ds(p, 1)] = row
        return carry

    lax.fori_loop(0, pairs, far_cut, 0, unroll=4)

    width = 2 * length
    lanes2 = lax.broadcasted_iota(jnp.int32, (1, 2 * width), 1)
    base = jnp.where((lanes2 == 0) | (lanes2 == width + length), 1.0 / length, 0.0)

    def spectra(ref, at, many):
        windows = ref[pl.ds(at, many)].reshape(many * length, cols)
        section = jnp.dot(windows, forward[...], preferred_element_type=F32)
        stacked = []
        for w in range(many):
            part = section[w * length:(w + 1) * length]
            part = (part - jnp.sum(part, axis=0, keepdims=True) * base).astype(BF16)
            stacked.append(jnp.concatenate([part[:, :width], part[:, width:]], axis=0))
        return jnp.dot(
            rows[...], jnp.concatenate(stacked, axis=1), preferred_element_type=F32
        )

    many = batch * chips

    def near_turn(t, carry):
        found = spectra(near, t * many, many)
        for w in range(many):
            value = found[:, w * width:(w + 1) * width]
            both = jnp.concatenate([value, pltpu.roll(value, length, 1)], axis=1)
            spec[t * many + w] = both.astype(BF16)
        return carry

    lax.fori_loop(0, dates // batch, near_turn, 0)

    steps = lax.broadcasted_iota(jnp.int32, (width, 1), 0)
    down_k = jnp.where(steps < length, steps, steps - width).astype(F32) * 0.5
    down_k = jnp.broadcast_to(down_k, (width, width))

    def turn(t, carry):
        found = spectra(far, t * many, many).astype(BF16)
        crossed = []
        for b in range(batch):
            day = first_s[t * batch + b]
            for c in range(chips):
                w = b * chips + c
                value = found[:, w * width:(w + 1) * width]
                crossed.append(spec[day * chips + c] * jnp.concatenate([value, value], axis=1))
        along = jnp.dot(
            jnp.concatenate(crossed, axis=0), back[...], preferred_element_type=F32
        ).astype(BF16)
        stacked = []
        for w in range(many):
            part = along[w * length:(w + 1) * length]
            stacked.append(jnp.concatenate([part[:, :width], part[:, width:]], axis=0))
        surface = jnp.dot(
            final[...], jnp.concatenate(stacked, axis=1), preferred_element_type=F32
        )
        for b in range(batch):
            for c in range(chips):
                w = b * chips + c
                value = surface[:, w * width:(w + 1) * width]
                energy = value * value
                at = (c, pl.ds(t * batch + b, 1))
                sums[at] = jnp.sum(energy, axis=0, keepdims=True)
                moments[at] = jnp.sum(energy * down_k, axis=0, keepdims=True)
        return carry

    lax.fori_loop(0, pairs // batch, turn, 0)

    across = lax.broadcasted_iota(jnp.int32, (pairs, width), 1)
    across = jnp.where(across < length, across, across - width).astype(F32) * 0.5
    live = lax.broadcasted_iota(jnp.int32, (pairs, 1), 0) < count_s[0]
    cells = 1.0 / (width * width)
    shift_all = moves[...]
    spot = lax.broadcasted_iota(jnp.int32, (pairs, partial_out.shape[1]), 1).astype(F32)
    spread = (spot == shift_all[:, 2 * chips:2 * chips + 1]).astype(F32) - (
        spot == shift_all[:, 2 * chips + 1:2 * chips + 2]
    ).astype(F32)
    columns = [None] * (2 * chips)
    for c in range(chips):
        held = sums[c]
        scale = jnp.sum(held, axis=1, keepdims=True) * cells + 1e-6
        low = jnp.sum(moments[c], axis=1, keepdims=True) * cells
        side = jnp.sum(held * across, axis=1, keepdims=True) * cells
        for x, value in enumerate((low, side)):
            k = x * chips + c
            columns[k] = jnp.where(live, shift_all[:, k:k + 1] + value / scale, 0.0)
    place = lax.broadcasted_iota(jnp.int32, (pairs, width), 1)
    table = jnp.zeros((pairs, width), F32)
    for k, column in enumerate(columns):
        table = jnp.where(place == k, column, table)
        partial_out[k:k + 1] = jnp.sum(column * spread, axis=0, keepdims=True)
    turned_table = jnp.transpose(table)
    for x in range(2):
        offsets_out[x] = turned_table[x * chips:(x + 1) * chips]


def series_kernel(n, partial, inverse, series_out, held, send, recv):
    me = lax.axis_index("date")
    peers = [lax.rem(me + j, n) for j in range(1, n)]
    barrier = pltpu.get_barrier_semaphore()
    for peer in peers:
        pl.semaphore_signal(barrier, inc=1, device_id={"date": peer}, device_id_type=MESH)
    pl.semaphore_wait(barrier, n - 1)
    copies = []
    for j, peer in enumerate(peers):
        copies.append(
            pltpu.make_async_remote_copy(
                src_ref=partial,
                dst_ref=held.at[j],
                send_sem=send.at[j],
                recv_sem=recv.at[j],
                device_id={"date": peer},
                device_id_type=MESH,
            )
        )
        copies[-1].start()
    total = partial[...]
    for copy in copies:
        copy.wait_recv()
    for j in range(n - 1):
        total = total + held[j]
    rows = inverse.shape[0]
    for k in range(rows):
        value = jnp.sum(inverse[k] * total[k:k + 1], axis=1)[None]
        chips = series_out.shape[1]
        series_out[k // chips, k % chips:k % chips + 1] = value
    for copy in copies:
        copy.wait_send()


def body(n, strips, images, inverse, first, block, second, count, shifts, anchors):
    dates, length, cols = images.shape
    pairs, chips = first.shape[0], anchors.shape[0]
    vmem, smem = pl.BlockSpec(memory_space=pltpu.VMEM), pl.BlockSpec(memory_space=pltpu.SMEM)
    top = images[:, :SMAX].reshape(dates * SMAX, cols)
    bot = images[:, length - SMAX:].reshape(dates * SMAX, cols)
    tables = make_tables(length)
    kinds = 30 if n == 8 else 2 * n
    grid, halo = pl.pallas_call(
        functools.partial(gather_kernel, n, strips),
        name="gather",
        out_shape=(
            jax.ShapeDtypeStruct((n, dates, length, cols), BF16),
            jax.ShapeDtypeStruct((n, 2, dates * SMAX, cols), BF16),
        ),
        in_specs=[vmem] * 3,
        out_specs=(vmem, vmem),
        scratch_shapes=[
            pltpu.SemaphoreType.DMA((1,)),
            pltpu.SemaphoreType.DMA((kinds,)),
            pltpu.SemaphoreType.DMA((kinds,)),
        ],
        compiler_params=pltpu.CompilerParams(collective_id=0, has_side_effects=True),
    )(images, top, bot)
    width = 2 * length
    batch = 4
    offsets, partial = pl.pallas_call(
        functools.partial(pairs_kernel, n, strips, batch),
        name="pairs",
        out_shape=(
            jax.ShapeDtypeStruct((2, chips, pairs), F32),
            jax.ShapeDtypeStruct((2 * chips, n * dates), F32),
        ),
        in_specs=[smem] * 6 + [vmem] * 7,
        out_specs=(vmem, vmem),
        scratch_shapes=[
            pltpu.VMEM((pairs, length + 2 * SMAX, cols), F32),
            pltpu.VMEM((pairs * chips, length, cols), BF16),
            pltpu.VMEM((dates * chips, length, cols), BF16),
            pltpu.VMEM((dates * chips, length, 2 * width), BF16),
            pltpu.VMEM((chips, pairs, width), F32),
            pltpu.VMEM((chips, pairs, width), F32),
            pltpu.VMEM((pairs, cols), F32),
        ],
    )(
        first, block.reshape(pairs), second, count, jnp.transpose(shifts, (1, 2, 0)), anchors,
        images,
        grid.reshape(n * dates, length, cols),
        halo.reshape(n * dates, 2 * SMAX, cols),
        *tables,
    )
    share = inverse.shape[2]
    series = pl.pallas_call(
        functools.partial(series_kernel, n),
        name="series",
        out_shape=jax.ShapeDtypeStruct((2, chips, share), F32),
        in_specs=[vmem, vmem],
        out_specs=vmem,
        scratch_shapes=[
            pltpu.VMEM((n - 1, 2 * chips, n * dates), F32),
            pltpu.SemaphoreType.DMA((n - 1,)),
            pltpu.SemaphoreType.DMA((n - 1,)),
        ],
        compiler_params=pltpu.CompilerParams(collective_id=1, has_side_effects=True),
    )(partial, inverse.reshape(2 * chips, share, n * dates))
    return jnp.transpose(offsets, (2, 0, 1)), series


def solution(mesh):
    return jax.shard_map(
        functools.partial(body, mesh.shape["date"], mesh.shape["strip"]),
        mesh=mesh,
        in_specs=(
            P("date", "strip", None),
            P(None, "strip", "date", None),
            P("date"),
            P("date", None),
            P("date"),
            P("date"),
            P("date", None, "strip"),
            P("strip"),
        ),
        out_specs=(P("date", None, "strip"), P(None, "strip", "date")),
        check_vma=False,
    )
```

```python
import functools
import math

import jax
import jax.numpy as jnp
import numpy as np
from jax import lax
from jax.experimental import pallas as pl
from jax.experimental.pallas import tpu as pltpu
from jax.sharding import PartitionSpec as P

SMAX = 8
MESH = pl.DeviceIdType.MESH
F32, BF16 = jnp.float32, jnp.bfloat16


def make_tables(length):
    counter = np.arange(length)
    radians = (counter[:, None] * counter[None, :] % length) * (2.0 * math.pi / length)
    cosine, sine = np.cos(radians), -np.sin(radians)
    over = 2 * length
    signed = np.where(counter < length // 2, counter, counter - length)
    places = np.arange(over)
    angles = (signed[:, None] * places[None, :] % over) * (2.0 * math.pi / over)
    vcos, vsin = np.cos(angles), np.sin(angles)
    forward = np.concatenate([cosine, sine, -sine, cosine], axis=1)
    forward = np.concatenate([forward, np.zeros_like(forward)], axis=0)
    rows = np.concatenate([cosine, sine], axis=1)
    one = np.concatenate([vcos, vsin], axis=1)
    two = np.concatenate([-vsin, vcos], axis=1)
    back = np.concatenate([one, one, two, -two], axis=0)
    final = np.concatenate([vcos.T, -vsin.T], axis=1)
    return [jnp.asarray(t.astype(np.float32)).astype(BF16) for t in (forward, rows, back, final)]


def exchange(n, strips, img, grid, halo, local, send, recv):
    me, strip = lax.axis_index("date"), lax.axis_index("strip")
    up, down = lax.rem(strip + strips - 1, strips), lax.rem(strip + 1, strips)
    dates, length = img.shape[:2]
    half = dates // 2
    first, second = pl.ds(0, half), pl.ds(half, dates - half)
    peers = [lax.rem(me + j, n) for j in range(1, n)]

    def sent(k, src, dst, where):
        return pltpu.make_async_remote_copy(
            src_ref=src,
            dst_ref=dst,
            send_sem=send.at[k],
            recv_sem=recv.at[k],
            device_id=where,
            device_id_type=MESH,
        )

    barrier = pltpu.get_barrier_semaphore()
    for peer in peers:
        pl.semaphore_signal(barrier, inc=1, device_id={"date": peer}, device_id_type=MESH)
    for other in (up, down):
        pl.semaphore_signal(barrier, inc=1, device_id={"strip": other}, device_id_type=MESH)
    own = pltpu.make_async_copy(img, grid.at[me], local.at[0])
    own.start()
    pl.semaphore_wait(barrier, n + 1)

    top, bot = img.at[:, pl.ds(0, SMAX)], img.at[:, pl.ds(length - SMAX, SMAX)]
    z_up = sent(0, top, halo.at[me, 0], {"strip": up})
    z_down = sent(1, bot, halo.at[me, 1], {"strip": down})
    if n != 8:
        z_up.start()
        z_down.start()
        copies = []
        for j, peer in enumerate(peers):
            copies.append(sent(2 + j, img, grid.at[me], {"date": peer}))
            copies[-1].start()
        z_up.wait()
        z_down.wait()
        for j, peer in enumerate(peers):
            copies.append(sent(n + 1 + j, halo.at[me], halo.at[me], {"date": peer}))
            copies[-1].start()
        yield
        yield
        yield
        for copy in copies:
            copy.wait()
        own.wait()
        return

    core, ex, wy = ({"date": jnp.bitwise_xor(me, j)} for j in (1, 2, 4))

    def family(base, own_ref, out, one, two):
        def made(k, block, part, where, mine=False):
            src = own_ref.at[part] if mine else out.at[block, part]
            return sent(base + k, src, out.at[block, part], where)

        near_x, near_y, diag = (jnp.bitwise_xor(me, j) for j in (2, 4, 6))
        return [
            made(0, me, one, wy, True),
            made(1, me, two, wy, True),
            made(2, me, two, ex, True),
            made(3, me, one, ex, True),
            made(4, me, one, core, True),
            made(5, near_y, one, ex),
            made(6, near_y, one, core),
            made(7, near_x, two, wy),
            made(8, near_x, two, core),
            made(9, near_y, two, core),
            made(10, near_x, one, core),
            made(11, diag, one, core),
            made(12, diag, two, core),
            made(13, me, two, core, True),
        ]

    main = family(2, img, grid, first, second)
    edge = family(16, halo.at[me], halo, 0, 1)

    def run(copies, ids):
        for k in ids:
            copies[k].start()

    run(main, (0, 2))
    z_up.start()
    z_down.start()
    run(main, (1, 3, 4, 13))
    yield
    z_up.wait_recv()
    z_down.wait_recv()
    run(edge, (0, 2, 1, 3, 4, 13))
    main[0].wait_recv()
    run(main, (5, 6))
    main[2].wait_recv()
    run(main, (7, 8))
    yield
    main[1].wait_recv()
    run(main, (9,))
    main[3].wait_recv()
    run(main, (10,))
    edge[0].wait_recv()
    run(edge, (5, 6))
    edge[2].wait_recv()
    run(edge, (7, 8))
    edge[1].wait_recv()
    run(edge, (9,))
    edge[3].wait_recv()
    run(edge, (10,))
    yield
    main[5].wait_recv()
    run(main, (11,))
    main[7].wait_recv()
    run(main, (12,))
    edge[5].wait_recv()
    run(edge, (11,))
    edge[7].wait_recv()
    run(edge, (12,))
    for k in (4, 13, 6, 8, 9, 10, 11, 12):
        main[k].wait_recv()
        edge[k].wait_recv()
    for copy in main + edge + [z_up, z_down]:
        copy.wait_send()
    own.wait()


def pairs_kernel(
    n, strips, batch,
    first_s, block_s, second_s, count_s, shifts_s, anchors_s,
    img, forward, rows, back, final,
    offsets_out, total_out,
    grid_in, halo_in, partial, held_sums, local, send, recv,
    wide, far, near, spec, sums, moments, moves,
):
    dates, length, cols = img.shape
    pairs, chips = first_s.shape[0], anchors_s.shape[0]
    me, strip = lax.axis_index("date"), lax.axis_index("strip")
    lane = lax.broadcasted_iota(jnp.int32, (length, cols), 1)
    has_up, has_down = strip > 0, strip < strips - 1
    moving = exchange(n, strips, img, grid_in, halo_in, local, send, recv)
    next(moving)

    def turned(value, start):
        rolled = pltpu.roll(value, lax.rem(2 * cols - start, cols), 1)
        inside = (lane >= -start) & (lane < cols - start)
        return jnp.where(inside, rolled, 0.0).astype(BF16)

    def near_cut(d, carry):
        value = img[d].astype(F32)
        for c in range(chips):
            near[d * chips + c] = turned(value, anchors_s[c])
        return carry

    lax.fori_loop(0, dates, near_cut, 0, unroll=4)

    def far_cut(p, carry):
        block, day = block_s[p], second_s[p]
        wide[p, pl.ds(SMAX, length)] = grid_in[block, day].astype(F32)
        for side, at, has in ((0, SMAX + length, has_down), (1, 0, has_up)):
            edge = halo_in[block, side, day].astype(F32)
            wide[p, pl.ds(at, SMAX)] = jnp.where(has, edge, 0.0)
        for c in range(chips):
            value = wide[p, pl.ds(SMAX + shifts_s[0, c, p], length)]
            far[p * chips + c] = turned(value, anchors_s[c] + shifts_s[1, c, p])
        place = lax.broadcasted_iota(jnp.int32, (1, cols), 1)
        row = jnp.zeros((1, cols), F32)
        for x in range(2):
            for c in range(chips):
                row = jnp.where(place == x * chips + c, shifts_s[x, c, p].astype(F32), row)
        row = jnp.where(place == 2 * chips, (block * dates + day).astype(F32), row)
        row = jnp.where(place == 2 * chips + 1, (me * dates + first_s[p]).astype(F32), row)
        moves[pl.ds(p, 1)] = row
        return carry

    width = 2 * length
    lanes2 = lax.broadcasted_iota(jnp.int32, (1, 2 * width), 1)
    base = jnp.where((lanes2 == 0) | (lanes2 == width + length), 1.0 / length, 0.0)

    def spectra(ref, at, many):
        windows = ref[pl.ds(at, many)].reshape(many * length, cols)
        section = jnp.dot(windows, forward[...], preferred_element_type=F32)
        stacked = []
        for w in range(many):
            part = section[w * length:(w + 1) * length]
            part = (part - jnp.sum(part, axis=0, keepdims=True) * base).astype(BF16)
            stacked.append(jnp.concatenate([part[:, :width], part[:, width:]], axis=0))
        return jnp.dot(
            rows[...], jnp.concatenate(stacked, axis=1), preferred_element_type=F32
        )

    many = batch * chips

    def near_turn(t, carry):
        found = spectra(near, t * many, many)
        for w in range(many):
            value = found[:, w * width:(w + 1) * width]
            both = jnp.concatenate([value, pltpu.roll(value, length, 1)], axis=1)
            spec[t * many + w] = both.astype(BF16)
        return carry

    rounds = dates // batch
    next(moving)
    lax.fori_loop(0, rounds // 2, near_turn, 0)
    next(moving)
    lax.fori_loop(rounds // 2, rounds, near_turn, 0)
    for _ in moving:
        pass
    lax.fori_loop(0, pairs, far_cut, 0, unroll=4)

    steps = lax.broadcasted_iota(jnp.int32, (width, 1), 0)
    down_k = jnp.where(steps < length, steps, steps - width).astype(F32) * 0.5
    down_k = jnp.broadcast_to(down_k, (width, width))

    def turn(t, carry):
        found = spectra(far, t * many, many).astype(BF16)
        crossed = []
        for b in range(batch):
            day = first_s[t * batch + b]
            for c in range(chips):
                w = b * chips + c
                value = found[:, w * width:(w + 1) * width]
                crossed.append(spec[day * chips + c] * jnp.concatenate([value, value], axis=1))
        along = jnp.dot(
            jnp.concatenate(crossed, axis=0), back[...], preferred_element_type=F32
        ).astype(BF16)
        stacked = []
        for w in range(many):
            part = along[w * length:(w + 1) * length]
            stacked.append(jnp.concatenate([part[:, :width], part[:, width:]], axis=0))
        surface = jnp.dot(
            final[...], jnp.concatenate(stacked, axis=1), preferred_element_type=F32
        )
        for b in range(batch):
            for c in range(chips):
                w = b * chips + c
                value = surface[:, w * width:(w + 1) * width]
                energy = value * value
                at = (c, pl.ds(t * batch + b, 1))
                sums[at] = jnp.sum(energy, axis=0, keepdims=True)
                moments[at] = jnp.sum(energy * down_k, axis=0, keepdims=True)
        return carry

    lax.fori_loop(0, pairs // batch, turn, 0)

    across = lax.broadcasted_iota(jnp.int32, (pairs, width), 1)
    across = jnp.where(across < length, across, across - width).astype(F32) * 0.5
    live = lax.broadcasted_iota(jnp.int32, (pairs, 1), 0) < count_s[0]
    cells = 1.0 / (width * width)
    shift_all = moves[...]
    spot = lax.broadcasted_iota(jnp.int32, (pairs, partial.shape[1]), 1).astype(F32)
    spread = (spot == shift_all[:, 2 * chips:2 * chips + 1]).astype(F32) - (
        spot == shift_all[:, 2 * chips + 1:2 * chips + 2]
    ).astype(F32)
    columns = [None] * (2 * chips)
    for c in range(chips):
        held = sums[c]
        scale = jnp.sum(held, axis=1, keepdims=True) * cells + 1e-6
        low = jnp.sum(moments[c], axis=1, keepdims=True) * cells
        side = jnp.sum(held * across, axis=1, keepdims=True) * cells
        for x, value in enumerate((low, side)):
            k = x * chips + c
            columns[k] = jnp.where(live, shift_all[:, k:k + 1] + value / scale, 0.0)
    place = lax.broadcasted_iota(jnp.int32, (pairs, width), 1)
    table = jnp.zeros((pairs, width), F32)
    for k, column in enumerate(columns):
        table = jnp.where(place == k, column, table)
        partial[k:k + 1] = jnp.sum(column * spread, axis=0, keepdims=True)
    turned_table = jnp.transpose(table)
    for x in range(2):
        offsets_out[x] = turned_table[x * chips:(x + 1) * chips]

    peers = [lax.rem(me + j, n) for j in range(1, n)]
    copies = []
    for j, peer in enumerate(peers):
        copies.append(
            pltpu.make_async_remote_copy(
                src_ref=partial,
                dst_ref=held_sums.at[j],
                send_sem=send.at[send.shape[0] - n + 1 + j],
                recv_sem=recv.at[recv.shape[0] - n + 1 + j],
                device_id={"date": peer},
                device_id_type=MESH,
            )
        )
        copies[-1].start()
    total = partial[...]
    for j, copy in enumerate(copies):
        copy.wait_recv()
        total = total + held_sums[j]
    total_out[...] = total
    for copy in copies:
        copy.wait_send()


def series_kernel(total, inverse, offsets, series_out, offsets_out):
    offsets_out[...] = offsets[...]
    chips = series_out.shape[1]
    for k in range(inverse.shape[0]):
        value = jnp.sum(inverse[k] * total[k:k + 1], axis=1)[None]
        series_out[k // chips, k % chips:k % chips + 1] = value


def body(n, strips, images, inverse, first, block, second, count, shifts, anchors):
    dates, length, cols = images.shape
    pairs, chips = first.shape[0], anchors.shape[0]
    vmem, smem = pl.BlockSpec(memory_space=pltpu.VMEM), pl.BlockSpec(memory_space=pltpu.SMEM)
    tables = make_tables(length)
    kinds = (30 if n == 8 else 2 * n) + n - 1
    width = 2 * length
    batch = 4
    offsets, total = pl.pallas_call(
        functools.partial(pairs_kernel, n, strips, batch),
        name="pairs",
        out_shape=(
            jax.ShapeDtypeStruct((2, chips, pairs), F32),
            jax.ShapeDtypeStruct((2 * chips, n * dates), F32),
        ),
        in_specs=[smem] * 6 + [vmem] * 5,
        out_specs=(vmem, vmem),
        scratch_shapes=[
            pltpu.VMEM((n, dates, length, cols), BF16),
            pltpu.VMEM((n, 2, dates, SMAX, cols), BF16),
            pltpu.VMEM((2 * chips, n * dates), F32),
            pltpu.VMEM((n - 1, 2 * chips, n * dates), F32),
            pltpu.SemaphoreType.DMA((1,)),
            pltpu.SemaphoreType.DMA((kinds,)),
            pltpu.SemaphoreType.DMA((kinds,)),
            pltpu.VMEM((pairs, length + 2 * SMAX, cols), F32),
            pltpu.VMEM((pairs * chips, length, cols), BF16),
            pltpu.VMEM((dates * chips, length, cols), BF16),
            pltpu.VMEM((dates * chips, length, 2 * width), BF16),
            pltpu.VMEM((chips, pairs, width), F32),
            pltpu.VMEM((chips, pairs, width), F32),
            pltpu.VMEM((pairs, cols), F32),
        ],
        compiler_params=pltpu.CompilerParams(collective_id=0, has_side_effects=True),
    )(
        first, block.reshape(pairs), second, count, jnp.transpose(shifts, (1, 2, 0)), anchors,
        images, *tables,
    )
    share = inverse.shape[2]
    series, offsets = pl.pallas_call(
        series_kernel,
        name="series",
        out_shape=(
            jax.ShapeDtypeStruct((2, chips, share), F32),
            jax.ShapeDtypeStruct((2, chips, pairs), F32),
        ),
        in_specs=[vmem] * 3,
        out_specs=(vmem, vmem),
    )(total, inverse.reshape(2 * chips, share, n * dates), offsets)
    return jnp.transpose(offsets, (2, 0, 1)), series


def solution(mesh):
    return jax.shard_map(
        functools.partial(body, mesh.shape["date"], mesh.shape["strip"]),
        mesh=mesh,
        in_specs=(
            P("date", "strip", None),
            P(None, "strip", "date", None),
            P("date"),
            P("date", None),
            P("date"),
            P("date"),
            P("date", None, "strip"),
            P("strip"),
        ),
        out_specs=(P("date", None, "strip"), P(None, "strip", "date")),
        check_vma=False,
    )
```

```python
import functools
import math

import jax
import jax.numpy as jnp
import numpy as np
from jax import lax
from jax.experimental import pallas as pl
from jax.experimental.pallas import tpu as pltpu
from jax.sharding import PartitionSpec as P

SMAX = 8
MESH = pl.DeviceIdType.MESH
F32, BF16 = jnp.float32, jnp.bfloat16


def make_tables(length):
    counter = np.arange(length)
    radians = (counter[:, None] * counter[None, :] % length) * (2.0 * math.pi / length)
    cosine, sine = np.cos(radians), -np.sin(radians)
    over = 2 * length
    signed = np.where(counter < length // 2, counter, counter - length)
    places = np.arange(over)
    angles = (signed[:, None] * places[None, :] % over) * (2.0 * math.pi / over)
    vcos, vsin = np.cos(angles), np.sin(angles)
    forward = np.concatenate([cosine, sine, -sine, cosine], axis=1)
    forward = np.concatenate([forward, np.zeros_like(forward)], axis=0)
    rows = np.concatenate([cosine, sine], axis=1)
    one = np.concatenate([vcos, vsin], axis=1)
    two = np.concatenate([-vsin, vcos], axis=1)
    back = np.concatenate([one, one, two, -two], axis=0)
    final = np.concatenate([vcos.T, -vsin.T], axis=1)
    return [jnp.asarray(t.astype(np.float32)).astype(BF16) for t in (forward, rows, back, final)]


def exchange(n, strips, img, tables, grid, halo, local, send, recv):
    me, strip = lax.axis_index("date"), lax.axis_index("strip")
    up, down = lax.max(strip - 1, 0), lax.min(strip + 1, strips - 1)
    dates, length = grid.shape[1:3]
    half = dates // 2
    first, second = pl.ds(0, half), pl.ds(half, dates - half)
    if n == 8:
        peers = [jnp.bitwise_xor(me, j) for j in (1, 2, 4)]
    else:
        peers = [lax.rem(me + j, n) for j in range(1, n)]
    has_up, has_down = strip > 0, strip < strips - 1

    def sent(k, src, dst, where):
        return pltpu.make_async_remote_copy(
            src_ref=src,
            dst_ref=dst,
            send_sem=send.at[k],
            recv_sem=recv.at[k],
            device_id=where,
            device_id_type=MESH,
        )

    barrier = pltpu.get_barrier_semaphore()
    for peer in peers:
        pl.semaphore_signal(barrier, inc=1, device_id={"date": peer}, device_id_type=MESH)
    for other, has in ((up, has_up), (down, has_down)):
        @pl.when(has)
        def _():
            pl.semaphore_signal(barrier, inc=1, device_id={"strip": other}, device_id_type=MESH)
    own = pltpu.make_async_copy(img, grid.at[me], local.at[0])
    own.start()
    loads = [pltpu.make_async_copy(a, b, local.at[1 + k]) for k, (a, b) in enumerate(tables)]
    for load in loads:
        load.start()
    for side, has in ((0, has_down), (1, has_up)):
        @pl.when(jnp.logical_not(has))
        def _():
            halo[me, side] = jnp.zeros(halo.shape[2:], halo.dtype)
    pl.semaphore_wait(barrier, len(peers) + has_up.astype(jnp.int32) + has_down.astype(jnp.int32))

    top, bot = img.at[:, pl.ds(0, SMAX)], img.at[:, pl.ds(length - SMAX, SMAX)]
    z_up = sent(0, top, halo.at[me, 0], {"strip": up})
    z_down = sent(1, bot, halo.at[me, 1], {"strip": down})

    def start_z():
        pl.when(has_up)(z_up.start)
        pl.when(has_down)(z_down.start)

    def got_z():
        pl.when(has_down)(z_up.wait_recv)
        pl.when(has_up)(z_down.wait_recv)

    def left_z():
        pl.when(has_up)(z_up.wait_send)
        pl.when(has_down)(z_down.wait_send)

    def settle():
        own.wait()
        for load in loads:
            load.wait()

    if n != 8:
        start_z()
        copies = []
        for j, peer in enumerate(peers):
            copies.append(sent(2 + j, img, grid.at[me], {"date": peer}))
            copies[-1].start()
        got_z()
        left_z()
        for j, peer in enumerate(peers):
            copies.append(sent(n + 1 + j, halo.at[me], halo.at[me], {"date": peer}))
            copies[-1].start()
        settle()
        yield
        yield
        yield
        for copy in copies:
            copy.wait()
        return

    core, ex, wy = ({"date": jnp.bitwise_xor(me, j)} for j in (1, 2, 4))

    def family(base, own_ref, out, one, two):
        def made(k, block, part, where, mine=False):
            src = own_ref.at[part] if mine else out.at[block, part]
            return sent(base + k, src, out.at[block, part], where)

        near_x, near_y, diag = (jnp.bitwise_xor(me, j) for j in (2, 4, 6))
        return [
            made(0, me, one, wy, True),
            made(1, me, two, wy, True),
            made(2, me, two, ex, True),
            made(3, me, one, ex, True),
            made(4, me, one, core, True),
            made(5, near_y, one, ex),
            made(6, near_y, one, core),
            made(7, near_x, two, wy),
            made(8, near_x, two, core),
            made(9, near_y, two, core),
            made(10, near_x, one, core),
            made(11, diag, one, core),
            made(12, diag, two, core),
            made(13, me, two, core, True),
        ]

    main = family(2, img, grid, first, second)
    edge = family(16, halo.at[me], halo, 0, 1)

    def run(copies, ids):
        for k in ids:
            copies[k].start()

    run(main, (0, 2))
    start_z()
    run(main, (1, 3, 4, 13))
    settle()
    yield
    got_z()
    run(edge, (0, 2, 1, 3, 4, 13))
    main[0].wait_recv()
    run(main, (5, 6))
    main[2].wait_recv()
    run(main, (7, 8))
    yield
    main[1].wait_recv()
    run(main, (9,))
    main[3].wait_recv()
    run(main, (10,))
    edge[0].wait_recv()
    run(edge, (5, 6))
    edge[2].wait_recv()
    run(edge, (7, 8))
    edge[1].wait_recv()
    run(edge, (9,))
    edge[3].wait_recv()
    run(edge, (10,))
    yield
    main[5].wait_recv()
    run(main, (11,))
    main[7].wait_recv()
    run(main, (12,))
    edge[5].wait_recv()
    run(edge, (11,))
    edge[7].wait_recv()
    run(edge, (12,))
    for k in (4, 13, 6, 8, 9, 10, 11, 12):
        main[k].wait_recv()
        edge[k].wait_recv()
    for copy in main + edge:
        copy.wait_send()
    left_z()


def pairs_kernel(
    n, strips, batch,
    first_s, block_s, second_s, count_s, shifts_s, anchors_s,
    img, forward_in, rows_in, back_in, final_in,
    offsets_out, total_out,
    forward, rows, back, final, grid_in, halo_in, partial, held_sums, local, send, recv,
    wide, far, near, spec, sums, moments, moves,
):
    dates, length, cols = grid_in.shape[1:]
    pairs, chips = first_s.shape[0], anchors_s.shape[0]
    me, strip = lax.axis_index("date"), lax.axis_index("strip")
    lane = lax.broadcasted_iota(jnp.int32, (length, cols), 1)
    has_up, has_down = strip > 0, strip < strips - 1
    tables = ((forward_in, forward), (rows_in, rows), (back_in, back), (final_in, final))
    moving = exchange(n, strips, img, tables, grid_in, halo_in, local, send, recv)
    next(moving)

    def turned(value, start):
        rolled = pltpu.roll(value, lax.rem(2 * cols - start, cols), 1)
        inside = (lane >= -start) & (lane < cols - start)
        return jnp.where(inside, rolled, 0.0).astype(BF16)

    def near_cut(d, carry):
        value = grid_in[me, d].astype(F32)
        for c in range(chips):
            near[d * chips + c] = turned(value, anchors_s[c])
        return carry

    lax.fori_loop(0, dates, near_cut, 0, unroll=4)

    def far_cut(p, carry):
        block, day = block_s[p], second_s[p]
        wide[p, pl.ds(SMAX, length)] = grid_in[block, day].astype(F32)
        for side, at, has in ((0, SMAX + length, has_down), (1, 0, has_up)):
            edge = halo_in[block, side, day].astype(F32)
            wide[p, pl.ds(at, SMAX)] = jnp.where(has, edge, 0.0)
        for c in range(chips):
            value = wide[p, pl.ds(SMAX + shifts_s[0, c, p], length)]
            far[p * chips + c] = turned(value, anchors_s[c] + shifts_s[1, c, p])
        place = lax.broadcasted_iota(jnp.int32, (1, cols), 1)
        row = jnp.zeros((1, cols), F32)
        for x in range(2):
            for c in range(chips):
                row = jnp.where(place == x * chips + c, shifts_s[x, c, p].astype(F32), row)
        row = jnp.where(place == 2 * chips, (block * dates + day).astype(F32), row)
        row = jnp.where(place == 2 * chips + 1, (me * dates + first_s[p]).astype(F32), row)
        moves[pl.ds(p, 1)] = row
        return carry

    width = 2 * length
    lanes2 = lax.broadcasted_iota(jnp.int32, (1, 2 * width), 1)
    base = jnp.where((lanes2 == 0) | (lanes2 == width + length), 1.0 / length, 0.0)

    def spectra(ref, at, many):
        windows = ref[pl.ds(at, many)].reshape(many * length, cols)
        section = jnp.dot(windows, forward[...], preferred_element_type=F32)
        stacked = []
        for w in range(many):
            part = section[w * length:(w + 1) * length]
            part = (part - jnp.sum(part, axis=0, keepdims=True) * base).astype(BF16)
            stacked.append(jnp.concatenate([part[:, :width], part[:, width:]], axis=0))
        return jnp.dot(
            rows[...], jnp.concatenate(stacked, axis=1), preferred_element_type=F32
        )

    many = batch * chips

    def near_turn(t, carry):
        found = spectra(near, t * many, many)
        for w in range(many):
            value = found[:, w * width:(w + 1) * width]
            both = jnp.concatenate([value, pltpu.roll(value, length, 1)], axis=1)
            spec[t * many + w] = both.astype(BF16)
        return carry

    rounds = dates // batch
    next(moving)
    lax.fori_loop(0, rounds // 2, near_turn, 0)
    next(moving)
    lax.fori_loop(rounds // 2, rounds, near_turn, 0)
    for _ in moving:
        pass
    lax.fori_loop(0, pairs, far_cut, 0, unroll=4)

    steps = lax.broadcasted_iota(jnp.int32, (width, 1), 0)
    down_k = jnp.where(steps < length, steps, steps - width).astype(F32) * 0.5
    down_k = jnp.broadcast_to(down_k, (width, width))

    def turn(t, carry):
        found = spectra(far, t * many, many).astype(BF16)
        crossed = []
        for b in range(batch):
            day = first_s[t * batch + b]
            for c in range(chips):
                w = b * chips + c
                value = found[:, w * width:(w + 1) * width]
                crossed.append(spec[day * chips + c] * jnp.concatenate([value, value], axis=1))
        along = jnp.dot(
            jnp.concatenate(crossed, axis=0), back[...], preferred_element_type=F32
        ).astype(BF16)
        stacked = []
        for w in range(many):
            part = along[w * length:(w + 1) * length]
            stacked.append(jnp.concatenate([part[:, :width], part[:, width:]], axis=0))
        surface = jnp.dot(
            final[...], jnp.concatenate(stacked, axis=1), preferred_element_type=F32
        )
        for b in range(batch):
            for c in range(chips):
                w = b * chips + c
                value = surface[:, w * width:(w + 1) * width]
                energy = value * value
                at = (c, pl.ds(t * batch + b, 1))
                sums[at] = jnp.sum(energy, axis=0, keepdims=True)
                moments[at] = jnp.sum(energy * down_k, axis=0, keepdims=True)
        return carry

    lax.fori_loop(0, pairs // batch, turn, 0)

    across = lax.broadcasted_iota(jnp.int32, (pairs, width), 1)
    across = jnp.where(across < length, across, across - width).astype(F32) * 0.5
    live = lax.broadcasted_iota(jnp.int32, (pairs, 1), 0) < count_s[0]
    cells = 1.0 / (width * width)
    shift_all = moves[...]
    spot = lax.broadcasted_iota(jnp.int32, (pairs, partial.shape[1]), 1).astype(F32)
    spread = (spot == shift_all[:, 2 * chips:2 * chips + 1]).astype(F32) - (
        spot == shift_all[:, 2 * chips + 1:2 * chips + 2]
    ).astype(F32)
    columns = [None] * (2 * chips)
    for c in range(chips):
        held = sums[c]
        scale = jnp.sum(held, axis=1, keepdims=True) * cells + 1e-6
        low = jnp.sum(moments[c], axis=1, keepdims=True) * cells
        side = jnp.sum(held * across, axis=1, keepdims=True) * cells
        for x, value in enumerate((low, side)):
            k = x * chips + c
            columns[k] = jnp.where(live, shift_all[:, k:k + 1] + value / scale, 0.0)
    place = lax.broadcasted_iota(jnp.int32, (pairs, width), 1)
    table = jnp.zeros((pairs, width), F32)
    for k, column in enumerate(columns):
        table = jnp.where(place == k, column, table)
        partial[k:k + 1] = jnp.sum(column * spread, axis=0, keepdims=True)
    turned_table = jnp.transpose(table)
    for x in range(2):
        offsets_out[x] = turned_table[x * chips:(x + 1) * chips]

    peers = [lax.rem(me + j, n) for j in range(1, n)]
    copies = []
    for j, peer in enumerate(peers):
        copies.append(
            pltpu.make_async_remote_copy(
                src_ref=partial,
                dst_ref=held_sums.at[j],
                send_sem=send.at[send.shape[0] - n + 1 + j],
                recv_sem=recv.at[recv.shape[0] - n + 1 + j],
                device_id={"date": peer},
                device_id_type=MESH,
            )
        )
        copies[-1].start()
    total = partial[...]
    for j, copy in enumerate(copies):
        copy.wait_recv()
        total = total + held_sums[j]
    total_out[...] = total
    for copy in copies:
        copy.wait_send()


def series_kernel(total, inverse, offsets, series_out, offsets_out):
    offsets_out[...] = offsets[...]
    chips = series_out.shape[1]
    for k in range(inverse.shape[0]):
        value = jnp.sum(inverse[k] * total[k:k + 1], axis=1)[None]
        series_out[k // chips, k % chips:k % chips + 1] = value


def body(n, strips, images, inverse, first, block, second, count, shifts, anchors):
    dates, length, cols = images.shape
    pairs, chips = first.shape[0], anchors.shape[0]
    vmem, smem = pl.BlockSpec(memory_space=pltpu.VMEM), pl.BlockSpec(memory_space=pltpu.SMEM)
    tables = make_tables(length)
    kinds = (30 if n == 8 else 2 * n) + n - 1
    width = 2 * length
    batch = 4
    offsets, total = pl.pallas_call(
        functools.partial(pairs_kernel, n, strips, batch),
        name="pairs",
        out_shape=(
            jax.ShapeDtypeStruct((2, chips, pairs), F32),
            jax.ShapeDtypeStruct((2 * chips, n * dates), F32),
        ),
        in_specs=[smem] * 6 + [pl.BlockSpec(memory_space=pl.ANY)] * 5,
        out_specs=(vmem, vmem),
        scratch_shapes=[
            *[pltpu.VMEM(table.shape, BF16) for table in tables],
            pltpu.VMEM((n, dates, length, cols), BF16),
            pltpu.VMEM((n, 2, dates, SMAX, cols), BF16),
            pltpu.VMEM((2 * chips, n * dates), F32),
            pltpu.VMEM((n - 1, 2 * chips, n * dates), F32),
            pltpu.SemaphoreType.DMA((1 + len(tables),)),
            pltpu.SemaphoreType.DMA((kinds,)),
            pltpu.SemaphoreType.DMA((kinds,)),
            pltpu.VMEM((pairs, length + 2 * SMAX, cols), F32),
            pltpu.VMEM((pairs * chips, length, cols), BF16),
            pltpu.VMEM((dates * chips, length, cols), BF16),
            pltpu.VMEM((dates * chips, length, 2 * width), BF16),
            pltpu.VMEM((chips, pairs, width), F32),
            pltpu.VMEM((chips, pairs, width), F32),
            pltpu.VMEM((pairs, cols), F32),
        ],
        compiler_params=pltpu.CompilerParams(collective_id=0, has_side_effects=True),
    )(
        first, block.reshape(pairs), second, count, jnp.transpose(shifts, (1, 2, 0)), anchors,
        images, *tables,
    )
    share = inverse.shape[2]
    series, offsets = pl.pallas_call(
        series_kernel,
        name="series",
        out_shape=(
            jax.ShapeDtypeStruct((2, chips, share), F32),
            jax.ShapeDtypeStruct((2, chips, pairs), F32),
        ),
        in_specs=[vmem] * 3,
        out_specs=(vmem, vmem),
    )(total, inverse.reshape(2 * chips, share, n * dates), offsets)
    return jnp.transpose(offsets, (2, 0, 1)), series


def solution(mesh):
    return jax.shard_map(
        functools.partial(body, mesh.shape["date"], mesh.shape["strip"]),
        mesh=mesh,
        in_specs=(
            P("date", "strip", None),
            P(None, "strip", "date", None),
            P("date"),
            P("date", None),
            P("date"),
            P("date"),
            P("date", None, "strip"),
            P("strip"),
        ),
        out_specs=(P("date", None, "strip"), P(None, "strip", "date")),
        check_vma=False,
    )
```

```python
import functools
import math

import jax
import jax.numpy as jnp
import numpy as np
from jax import lax
from jax.experimental import pallas as pl
from jax.experimental.pallas import tpu as pltpu
from jax.sharding import PartitionSpec as P

SMAX = 8
MESH = pl.DeviceIdType.MESH
F32, BF16 = jnp.float32, jnp.bfloat16


def make_tables(length):
    counter = np.arange(length)
    radians = (counter[:, None] * counter[None, :] % length) * (2.0 * math.pi / length)
    cosine, sine = np.cos(radians), -np.sin(radians)
    over = 2 * length
    signed = np.where(counter < length // 2, counter, counter - length)
    places = np.arange(over)
    angles = (signed[:, None] * places[None, :] % over) * (2.0 * math.pi / over)
    vcos, vsin = np.cos(angles), np.sin(angles)
    forward = np.concatenate([cosine, sine, -sine, cosine], axis=1)
    forward = np.concatenate([forward, np.zeros_like(forward)], axis=0)
    rows = np.concatenate([cosine, sine], axis=1)
    one = np.concatenate([vcos, vsin], axis=1)
    two = np.concatenate([-vsin, vcos], axis=1)
    back = np.concatenate([one, one, two, -two], axis=0)
    final = np.concatenate([vcos.T, -vsin.T], axis=1)
    return [jnp.asarray(t.astype(np.float32)).astype(BF16) for t in (forward, rows, back, final)]


def exchange(n, strips, img, tables, grid, halo, local, send, recv):
    me, strip = lax.axis_index("date"), lax.axis_index("strip")
    up, down = lax.max(strip - 1, 0), lax.min(strip + 1, strips - 1)
    dates, length = grid.shape[1:3]
    half = dates // 2
    first, second = pl.ds(0, half), pl.ds(half, dates - half)
    if n == 8:
        peers = [jnp.bitwise_xor(me, j) for j in (1, 2, 4)]
    else:
        peers = [lax.rem(me + j, n) for j in range(1, n)]
    has_up, has_down = strip > 0, strip < strips - 1

    def sent(k, src, dst, where):
        return pltpu.make_async_remote_copy(
            src_ref=src,
            dst_ref=dst,
            send_sem=send.at[k],
            recv_sem=recv.at[k],
            device_id=where,
            device_id_type=MESH,
        )

    barrier = pltpu.get_barrier_semaphore()
    for peer in peers:
        pl.semaphore_signal(barrier, inc=1, device_id={"date": peer}, device_id_type=MESH)
    for other, has in ((up, has_up), (down, has_down)):
        @pl.when(has)
        def _():
            pl.semaphore_signal(barrier, inc=1, device_id={"strip": other}, device_id_type=MESH)
    own = pltpu.make_async_copy(img, grid.at[me], local.at[0])
    own.start()
    loads = [pltpu.make_async_copy(a, b, local.at[1 + k]) for k, (a, b) in enumerate(tables)]
    for load in loads:
        load.start()
    for side, has in ((0, has_down), (1, has_up)):
        @pl.when(jnp.logical_not(has))
        def _():
            halo[me, side] = jnp.zeros(halo.shape[2:], halo.dtype)
    pl.semaphore_wait(barrier, len(peers) + has_up.astype(jnp.int32) + has_down.astype(jnp.int32))

    top, bot = img.at[:, pl.ds(0, SMAX)], img.at[:, pl.ds(length - SMAX, SMAX)]
    z_up = sent(0, top, halo.at[me, 0], {"strip": up})
    z_down = sent(1, bot, halo.at[me, 1], {"strip": down})

    def start_z():
        pl.when(has_up)(z_up.start)
        pl.when(has_down)(z_down.start)

    def got_z():
        pl.when(has_down)(z_up.wait_recv)
        pl.when(has_up)(z_down.wait_recv)

    def left_z():
        pl.when(has_up)(z_up.wait_send)
        pl.when(has_down)(z_down.wait_send)

    def settle():
        own.wait()
        for load in loads:
            load.wait()

    if n != 8:
        start_z()
        copies = []
        for j, peer in enumerate(peers):
            copies.append(sent(2 + j, img, grid.at[me], {"date": peer}))
            copies[-1].start()
        got_z()
        left_z()
        for j, peer in enumerate(peers):
            copies.append(sent(n + 1 + j, halo.at[me], halo.at[me], {"date": peer}))
            copies[-1].start()
        settle()
        yield
        yield
        yield
        for copy in copies:
            copy.wait()
        return

    core, ex, wy = ({"date": jnp.bitwise_xor(me, j)} for j in (1, 2, 4))

    def family(base, own_ref, out, one, two):
        def made(k, block, part, where, mine=False):
            src = own_ref.at[part] if mine else out.at[block, part]
            return sent(base + k, src, out.at[block, part], where)

        near_x, near_y, diag = (jnp.bitwise_xor(me, j) for j in (2, 4, 6))
        return [
            made(0, me, one, wy, True),
            made(1, me, two, wy, True),
            made(2, me, two, ex, True),
            made(3, me, one, ex, True),
            made(4, me, one, core, True),
            made(5, near_y, one, ex),
            made(6, near_y, one, core),
            made(7, near_x, two, wy),
            made(8, near_x, two, core),
            made(9, near_y, two, core),
            made(10, near_x, one, core),
            made(11, diag, one, core),
            made(12, diag, two, core),
            made(13, me, two, core, True),
        ]

    main = family(2, img, grid, first, second)
    edge = family(16, halo.at[me], halo, 0, 1)

    def run(copies, ids):
        for k in ids:
            copies[k].start()

    run(main, (0, 2))
    start_z()
    run(main, (1, 3, 4, 13))
    settle()
    yield
    got_z()
    run(edge, (0, 2, 1, 3, 4, 13))
    main[0].wait_recv()
    run(main, (5, 6))
    main[2].wait_recv()
    run(main, (7, 8))
    yield
    main[1].wait_recv()
    run(main, (9,))
    main[3].wait_recv()
    run(main, (10,))
    edge[0].wait_recv()
    run(edge, (5, 6))
    edge[2].wait_recv()
    run(edge, (7, 8))
    edge[1].wait_recv()
    run(edge, (9,))
    edge[3].wait_recv()
    run(edge, (10,))
    yield
    main[5].wait_recv()
    run(main, (11,))
    main[7].wait_recv()
    run(main, (12,))
    edge[5].wait_recv()
    run(edge, (11,))
    edge[7].wait_recv()
    run(edge, (12,))
    for k in (4, 13, 6, 8, 9, 10, 11, 12):
        main[k].wait_recv()
        edge[k].wait_recv()
    for copy in main + edge:
        copy.wait_send()
    left_z()


def pairs_kernel(
    n, strips, batch,
    first_s, block_s, second_s, count_s, shifts_s, anchors_s,
    img, forward_in, rows_in, back_in, final_in,
    offsets_out, total_out,
    forward, rows, back, final, grid_in, halo_in, partial, held_sums, local, send, recv,
    wide, far, near, spec, sums, moments, moves,
):
    dates, length, cols = grid_in.shape[1:]
    pairs, chips = first_s.shape[0], anchors_s.shape[0]
    me, strip = lax.axis_index("date"), lax.axis_index("strip")
    lane = lax.broadcasted_iota(jnp.int32, (length, cols), 1)
    has_up, has_down = strip > 0, strip < strips - 1
    tables = ((forward_in, forward), (rows_in, rows), (back_in, back), (final_in, final))
    moving = exchange(n, strips, img, tables, grid_in, halo_in, local, send, recv)
    next(moving)

    def turned(value, start):
        rolled = pltpu.roll(value, lax.rem(2 * cols - start, cols), 1)
        inside = (lane >= -start) & (lane < cols - start)
        return jnp.where(inside, rolled, 0.0).astype(BF16)

    def near_cut(d, carry):
        value = grid_in[me, d].astype(F32)
        for c in range(chips):
            near[d * chips + c] = turned(value, anchors_s[c])
        return carry

    lax.fori_loop(0, dates, near_cut, 0, unroll=8)

    def far_cut(p, carry):
        block, day = block_s[p], second_s[p]
        wide[p, pl.ds(SMAX, length)] = grid_in[block, day].astype(F32)
        for side, at, has in ((0, SMAX + length, has_down), (1, 0, has_up)):
            edge = halo_in[block, side, day].astype(F32)
            wide[p, pl.ds(at, SMAX)] = jnp.where(has, edge, 0.0)
        for c in range(chips):
            value = wide[p, pl.ds(SMAX + shifts_s[0, c, p], length)]
            far[p * chips + c] = turned(value, anchors_s[c] + shifts_s[1, c, p])
        place = lax.broadcasted_iota(jnp.int32, (1, cols), 1)
        row = jnp.zeros((1, cols), F32)
        for x in range(2):
            for c in range(chips):
                row = jnp.where(place == x * chips + c, shifts_s[x, c, p].astype(F32), row)
        row = jnp.where(place == 2 * chips, (block * dates + day).astype(F32), row)
        row = jnp.where(place == 2 * chips + 1, (me * dates + first_s[p]).astype(F32), row)
        moves[pl.ds(p, 1)] = row
        return carry

    width = 2 * length
    lanes2 = lax.broadcasted_iota(jnp.int32, (1, 2 * width), 1)
    base = jnp.where((lanes2 == 0) | (lanes2 == width + length), 1.0 / length, 0.0)

    def spectra(ref, at, many):
        windows = ref[pl.ds(at, many)].reshape(many * length, cols)
        section = jnp.dot(windows, forward[...], preferred_element_type=F32)
        stacked = []
        for w in range(many):
            part = section[w * length:(w + 1) * length]
            part = (part - jnp.sum(part, axis=0, keepdims=True) * base).astype(BF16)
            stacked.append(jnp.concatenate([part[:, :width], part[:, width:]], axis=0))
        return jnp.dot(
            rows[...], jnp.concatenate(stacked, axis=1), preferred_element_type=F32
        )

    many = batch * chips

    def near_turn(t, carry):
        found = spectra(near, t * many, many)
        for w in range(many):
            value = found[:, w * width:(w + 1) * width]
            both = jnp.concatenate([value, pltpu.roll(value, length, 1)], axis=1)
            spec[t * many + w] = both.astype(BF16)
        return carry

    rounds = dates // batch
    next(moving)
    lax.fori_loop(0, rounds // 2, near_turn, 0)
    next(moving)
    lax.fori_loop(rounds // 2, rounds, near_turn, 0)
    for _ in moving:
        pass
    lax.fori_loop(0, pairs, far_cut, 0, unroll=16)

    steps = lax.broadcasted_iota(jnp.int32, (width, 1), 0)
    down_k = jnp.where(steps < length, steps, steps - width).astype(F32) * 0.5
    down_k = jnp.broadcast_to(down_k, (width, width))

    def turn(t, carry):
        found = spectra(far, t * many, many).astype(BF16)
        crossed = []
        for b in range(batch):
            day = first_s[t * batch + b]
            for c in range(chips):
                w = b * chips + c
                value = found[:, w * width:(w + 1) * width]
                crossed.append(spec[day * chips + c] * jnp.concatenate([value, value], axis=1))
        along = jnp.dot(
            jnp.concatenate(crossed, axis=0), back[...], preferred_element_type=F32
        ).astype(BF16)
        stacked = []
        for w in range(many):
            part = along[w * length:(w + 1) * length]
            stacked.append(jnp.concatenate([part[:, :width], part[:, width:]], axis=0))
        surface = jnp.dot(
            final[...], jnp.concatenate(stacked, axis=1), preferred_element_type=F32
        )
        for b in range(batch):
            for c in range(chips):
                w = b * chips + c
                value = surface[:, w * width:(w + 1) * width]
                energy = value * value
                at = (c, pl.ds(t * batch + b, 1))
                sums[at] = jnp.sum(energy, axis=0, keepdims=True)
                moments[at] = jnp.sum(energy * down_k, axis=0, keepdims=True)
        return carry

    lax.fori_loop(0, pairs // batch, turn, 0)

    across = lax.broadcasted_iota(jnp.int32, (pairs, width), 1)
    across = jnp.where(across < length, across, across - width).astype(F32) * 0.5
    live = lax.broadcasted_iota(jnp.int32, (pairs, 1), 0) < count_s[0]
    cells = 1.0 / (width * width)
    shift_all = moves[...]
    spot = lax.broadcasted_iota(jnp.int32, (pairs, partial.shape[1]), 1).astype(F32)
    spread = (spot == shift_all[:, 2 * chips:2 * chips + 1]).astype(F32) - (
        spot == shift_all[:, 2 * chips + 1:2 * chips + 2]
    ).astype(F32)
    columns = [None] * (2 * chips)
    for c in range(chips):
        held = sums[c]
        scale = jnp.sum(held, axis=1, keepdims=True) * cells + 1e-6
        low = jnp.sum(moments[c], axis=1, keepdims=True) * cells
        side = jnp.sum(held * across, axis=1, keepdims=True) * cells
        for x, value in enumerate((low, side)):
            k = x * chips + c
            columns[k] = jnp.where(live, shift_all[:, k:k + 1] + value / scale, 0.0)
    place = lax.broadcasted_iota(jnp.int32, (pairs, width), 1)
    table = jnp.zeros((pairs, width), F32)
    for k, column in enumerate(columns):
        table = jnp.where(place == k, column, table)
        partial[k:k + 1] = jnp.sum(column * spread, axis=0, keepdims=True)
    turned_table = jnp.transpose(table)
    for x in range(2):
        offsets_out[x] = turned_table[x * chips:(x + 1) * chips]

    peers = [lax.rem(me + j, n) for j in range(1, n)]
    copies = []
    for j, peer in enumerate(peers):
        copies.append(
            pltpu.make_async_remote_copy(
                src_ref=partial,
                dst_ref=held_sums.at[j],
                send_sem=send.at[send.shape[0] - n + 1 + j],
                recv_sem=recv.at[recv.shape[0] - n + 1 + j],
                device_id={"date": peer},
                device_id_type=MESH,
            )
        )
        copies[-1].start()
    total = partial[...]
    for j, copy in enumerate(copies):
        copy.wait_recv()
        total = total + held_sums[j]
    total_out[...] = total
    for copy in copies:
        copy.wait_send()


def series_kernel(total, inverse, offsets, series_out, offsets_out):
    offsets_out[...] = offsets[...]
    chips = series_out.shape[1]
    for k in range(inverse.shape[0]):
        value = jnp.sum(inverse[k] * total[k:k + 1], axis=1)[None]
        series_out[k // chips, k % chips:k % chips + 1] = value


def body(n, strips, images, inverse, first, block, second, count, shifts, anchors):
    dates, length, cols = images.shape
    pairs, chips = first.shape[0], anchors.shape[0]
    vmem, smem = pl.BlockSpec(memory_space=pltpu.VMEM), pl.BlockSpec(memory_space=pltpu.SMEM)
    tables = make_tables(length)
    kinds = (30 if n == 8 else 2 * n) + n - 1
    width = 2 * length
    batch = math.gcd(16, math.gcd(pairs, dates))
    offsets, total = pl.pallas_call(
        functools.partial(pairs_kernel, n, strips, batch),
        name="pairs",
        out_shape=(
            jax.ShapeDtypeStruct((2, chips, pairs), F32),
            jax.ShapeDtypeStruct((2 * chips, n * dates), F32),
        ),
        in_specs=[smem] * 6 + [pl.BlockSpec(memory_space=pl.ANY)] * 5,
        out_specs=(vmem, vmem),
        scratch_shapes=[
            *[pltpu.VMEM(table.shape, BF16) for table in tables],
            pltpu.VMEM((n, dates, length, cols), BF16),
            pltpu.VMEM((n, 2, dates, SMAX, cols), BF16),
            pltpu.VMEM((2 * chips, n * dates), F32),
            pltpu.VMEM((n - 1, 2 * chips, n * dates), F32),
            pltpu.SemaphoreType.DMA((1 + len(tables),)),
            pltpu.SemaphoreType.DMA((kinds,)),
            pltpu.SemaphoreType.DMA((kinds,)),
            pltpu.VMEM((pairs, length + 2 * SMAX, cols), F32),
            pltpu.VMEM((pairs * chips, length, cols), BF16),
            pltpu.VMEM((dates * chips, length, cols), BF16),
            pltpu.VMEM((dates * chips, length, 2 * width), BF16),
            pltpu.VMEM((chips, pairs, width), F32),
            pltpu.VMEM((chips, pairs, width), F32),
            pltpu.VMEM((pairs, cols), F32),
        ],
        compiler_params=pltpu.CompilerParams(collective_id=0, has_side_effects=True),
    )(
        first, block.reshape(pairs), second, count, jnp.transpose(shifts, (1, 2, 0)), anchors,
        images, *tables,
    )
    share = inverse.shape[2]
    series, offsets = pl.pallas_call(
        series_kernel,
        name="series",
        out_shape=(
            jax.ShapeDtypeStruct((2, chips, share), F32),
            jax.ShapeDtypeStruct((2, chips, pairs), F32),
        ),
        in_specs=[vmem] * 3,
        out_specs=(vmem, vmem),
    )(total, inverse.reshape(2 * chips, share, n * dates), offsets)
    return jnp.transpose(offsets, (2, 0, 1)), series


def solution(mesh):
    return jax.shard_map(
        functools.partial(body, mesh.shape["date"], mesh.shape["strip"]),
        mesh=mesh,
        in_specs=(
            P("date", "strip", None),
            P(None, "strip", "date", None),
            P("date"),
            P("date", None),
            P("date"),
            P("date"),
            P("date", None, "strip"),
            P("strip"),
        ),
        out_specs=(P("date", None, "strip"), P(None, "strip", "date")),
        check_vma=False,
    )
```

```python
import functools
import math

import jax
import jax.numpy as jnp
import numpy as np
from jax import lax
from jax.experimental import pallas as pl
from jax.experimental.pallas import tpu as pltpu
from jax.sharding import PartitionSpec as P

SMAX = 8
MESH = pl.DeviceIdType.MESH
F32, BF16 = jnp.float32, jnp.bfloat16


def make_tables(length):
    counter = np.arange(length)
    radians = (counter[:, None] * counter[None, :] % length) * (2.0 * math.pi / length)
    cosine, sine = np.cos(radians), -np.sin(radians)
    over = 2 * length
    signed = np.where(counter < length // 2, counter, counter - length)
    places = np.arange(over)
    angles = (signed[:, None] * places[None, :] % over) * (2.0 * math.pi / over)
    vcos, vsin = np.cos(angles), np.sin(angles)
    forward = np.concatenate([cosine, sine, -sine, cosine], axis=1)
    forward = np.concatenate([forward, np.zeros_like(forward)], axis=0)
    rows = np.concatenate([cosine, sine], axis=1)
    one = np.concatenate([vcos, vsin], axis=1)
    two = np.concatenate([-vsin, vcos], axis=1)
    back = np.concatenate([one, one, two, -two], axis=0)
    final = np.concatenate([vcos.T, -vsin.T], axis=1)
    return [jnp.asarray(t.astype(np.float32)).astype(BF16) for t in (forward, rows, back, final)]


def exchange(n, strips, img, tables, grid, halo, local, send, recv):
    me, strip = lax.axis_index("date"), lax.axis_index("strip")
    up, down = lax.max(strip - 1, 0), lax.min(strip + 1, strips - 1)
    dates, length = grid.shape[1:3]
    half = dates // 2
    first, second = pl.ds(0, half), pl.ds(half, dates - half)
    if n == 8:
        peers = [jnp.bitwise_xor(me, j) for j in (1, 2, 4)]
    else:
        peers = [lax.rem(me + j, n) for j in range(1, n)]
    has_up, has_down = strip > 0, strip < strips - 1

    def sent(k, src, dst, where):
        return pltpu.make_async_remote_copy(
            src_ref=src,
            dst_ref=dst,
            send_sem=send.at[k],
            recv_sem=recv.at[k],
            device_id=where,
            device_id_type=MESH,
        )

    barrier = pltpu.get_barrier_semaphore()
    for peer in peers:
        pl.semaphore_signal(barrier, inc=1, device_id={"date": peer}, device_id_type=MESH)
    for other, has in ((up, has_up), (down, has_down)):
        @pl.when(has)
        def _():
            pl.semaphore_signal(barrier, inc=1, device_id={"strip": other}, device_id_type=MESH)
    own = pltpu.make_async_copy(img, grid.at[me], local.at[0])
    own.start()
    loads = [pltpu.make_async_copy(a, b, local.at[1 + k]) for k, (a, b) in enumerate(tables)]
    for load in loads:
        load.start()
    for side, has in ((0, has_down), (1, has_up)):
        @pl.when(jnp.logical_not(has))
        def _():
            halo[me, side] = jnp.zeros(halo.shape[2:], halo.dtype)
    pl.semaphore_wait(barrier, len(peers) + has_up.astype(jnp.int32) + has_down.astype(jnp.int32))

    top, bot = img.at[:, pl.ds(0, SMAX)], img.at[:, pl.ds(length - SMAX, SMAX)]
    z_up = sent(0, top, halo.at[me, 0], {"strip": up})
    z_down = sent(1, bot, halo.at[me, 1], {"strip": down})

    def start_z():
        pl.when(has_up)(z_up.start)
        pl.when(has_down)(z_down.start)

    def got_z():
        pl.when(has_down)(z_up.wait_recv)
        pl.when(has_up)(z_down.wait_recv)

    def left_z():
        pl.when(has_up)(z_up.wait_send)
        pl.when(has_down)(z_down.wait_send)

    def settle():
        own.wait()
        for load in loads:
            load.wait()

    if n != 8:
        start_z()
        copies = []
        for j, peer in enumerate(peers):
            copies.append(sent(2 + j, img, grid.at[me], {"date": peer}))
            copies[-1].start()
        got_z()
        left_z()
        for j, peer in enumerate(peers):
            copies.append(sent(n + 1 + j, halo.at[me], halo.at[me], {"date": peer}))
            copies[-1].start()
        settle()
        yield
        yield
        yield
        for copy in copies:
            copy.wait()
        return

    core, ex, wy = ({"date": jnp.bitwise_xor(me, j)} for j in (1, 2, 4))

    def family(base, own_ref, out, one, two):
        def made(k, block, part, where, mine=False):
            src = own_ref.at[part] if mine else out.at[block, part]
            return sent(base + k, src, out.at[block, part], where)

        near_x, near_y, diag = (jnp.bitwise_xor(me, j) for j in (2, 4, 6))
        return [
            made(0, me, one, wy, True),
            made(1, me, two, wy, True),
            made(2, me, two, ex, True),
            made(3, me, one, ex, True),
            made(4, me, one, core, True),
            made(5, near_y, one, ex),
            made(6, near_y, one, core),
            made(7, near_x, two, wy),
            made(8, near_x, two, core),
            made(9, near_y, two, core),
            made(10, near_x, one, core),
            made(11, diag, one, core),
            made(12, diag, two, core),
            made(13, me, two, core, True),
        ]

    main = family(2, img, grid, first, second)
    edge = family(16, halo.at[me], halo, 0, 1)

    def run(copies, ids):
        for k in ids:
            copies[k].start()

    run(main, (0, 2))
    start_z()
    run(main, (1, 3, 4, 13))
    settle()
    yield
    got_z()
    run(edge, (0, 2, 1, 3, 4, 13))
    main[0].wait_recv()
    run(main, (5, 6))
    main[2].wait_recv()
    run(main, (7, 8))
    yield
    main[1].wait_recv()
    run(main, (9,))
    main[3].wait_recv()
    run(main, (10,))
    edge[0].wait_recv()
    run(edge, (5, 6))
    edge[2].wait_recv()
    run(edge, (7, 8))
    edge[1].wait_recv()
    run(edge, (9,))
    edge[3].wait_recv()
    run(edge, (10,))
    yield
    main[5].wait_recv()
    run(main, (11,))
    main[7].wait_recv()
    run(main, (12,))
    edge[5].wait_recv()
    run(edge, (11,))
    edge[7].wait_recv()
    run(edge, (12,))
    for k in (4, 13, 6, 8, 9, 10, 11, 12):
        main[k].wait_recv()
        edge[k].wait_recv()
    for copy in main + edge:
        copy.wait_send()
    left_z()


def pairs_kernel(
    n, strips, batch,
    first_s, block_s, second_s, count_s, shifts_s, anchors_s,
    img, forward_in, rows_in, back_in, final_in,
    offsets_out, total_out,
    forward, rows, back, final, grid_in, halo_in, partial, held_sums, local, send, recv,
    wide, far, near, spec, sums, moments, moves,
):
    dates, length, cols = grid_in.shape[1:]
    pairs, chips = first_s.shape[0], anchors_s.shape[0]
    me, strip = lax.axis_index("date"), lax.axis_index("strip")
    lane = lax.broadcasted_iota(jnp.int32, (length, cols), 1)
    has_up, has_down = strip > 0, strip < strips - 1
    tables = ((forward_in, forward), (rows_in, rows), (back_in, back), (final_in, final))
    moving = exchange(n, strips, img, tables, grid_in, halo_in, local, send, recv)
    next(moving)

    def turned(value, start):
        rolled = pltpu.roll(value, lax.rem(2 * cols - start, cols), 1)
        inside = (lane >= -start) & (lane < cols - start)
        return jnp.where(inside, rolled, 0.0).astype(BF16)

    def near_cut(d, carry):
        value = grid_in[me, d].astype(F32)
        for c in range(chips):
            near[d * chips + c] = turned(value, anchors_s[c])
        return carry

    lax.fori_loop(0, dates, near_cut, 0, unroll=8)

    def far_cut(p, carry):
        block, day = block_s[p], second_s[p]
        wide[p, pl.ds(SMAX, length)] = grid_in[block, day].astype(F32)
        for side, at, has in ((0, SMAX + length, has_down), (1, 0, has_up)):
            edge = halo_in[block, side, day].astype(F32)
            wide[p, pl.ds(at, SMAX)] = jnp.where(has, edge, 0.0)
        for c in range(chips):
            value = wide[p, pl.ds(SMAX + shifts_s[0, c, p], length)]
            far[p * chips + c] = turned(value, anchors_s[c] + shifts_s[1, c, p])
        place = lax.broadcasted_iota(jnp.int32, (1, cols), 1)
        row = jnp.zeros((1, cols), F32)
        for x in range(2):
            for c in range(chips):
                row = jnp.where(place == x * chips + c, shifts_s[x, c, p].astype(F32), row)
        row = jnp.where(place == 2 * chips, (block * dates + day).astype(F32), row)
        row = jnp.where(place == 2 * chips + 1, (me * dates + first_s[p]).astype(F32), row)
        moves[pl.ds(p, 1)] = row
        return carry

    width = 2 * length
    lanes2 = lax.broadcasted_iota(jnp.int32, (1, 2 * width), 1)
    base = jnp.where((lanes2 == 0) | (lanes2 == width + length), 1.0 / length, 0.0)

    def spectra(ref, at, many):
        windows = ref[pl.ds(at, many)].reshape(many * length, cols)
        section = jnp.dot(windows, forward[...], preferred_element_type=F32)
        stacked = []
        for w in range(many):
            part = section[w * length:(w + 1) * length]
            part = (part - jnp.sum(part, axis=0, keepdims=True) * base).astype(BF16)
            stacked.append(jnp.concatenate([part[:, :width], part[:, width:]], axis=0))
        return jnp.dot(
            rows[...], jnp.concatenate(stacked, axis=1), preferred_element_type=F32
        )

    many = batch * chips

    def near_turn(t, carry):
        found = spectra(near, t * many, many)
        for w in range(many):
            value = found[:, w * width:(w + 1) * width]
            both = jnp.concatenate([value, pltpu.roll(value, length, 1)], axis=1)
            spec[t * many + w] = both.astype(BF16)
        return carry

    rounds = dates // batch
    next(moving)
    lax.fori_loop(0, rounds // 2, near_turn, 0)
    next(moving)
    lax.fori_loop(rounds // 2, rounds, near_turn, 0)
    for _ in moving:
        pass
    lax.fori_loop(0, pairs, far_cut, 0, unroll=32)

    steps = lax.broadcasted_iota(jnp.int32, (width, 1), 0)
    down_k = jnp.where(steps < length, steps, steps - width).astype(F32) * 0.5
    down_k = jnp.broadcast_to(down_k, (width, width))

    def turn(t, carry):
        found = spectra(far, t * many, many).astype(BF16)
        crossed = []
        for b in range(batch):
            day = first_s[t * batch + b]
            for c in range(chips):
                w = b * chips + c
                value = found[:, w * width:(w + 1) * width]
                crossed.append(spec[day * chips + c] * jnp.concatenate([value, value], axis=1))
        along = jnp.dot(
            jnp.concatenate(crossed, axis=0), back[...], preferred_element_type=F32
        ).astype(BF16)
        stacked = []
        for w in range(many):
            part = along[w * length:(w + 1) * length]
            stacked.append(jnp.concatenate([part[:, :width], part[:, width:]], axis=0))
        surface = jnp.dot(
            final[...], jnp.concatenate(stacked, axis=1), preferred_element_type=F32
        )
        for b in range(batch):
            for c in range(chips):
                w = b * chips + c
                value = surface[:, w * width:(w + 1) * width]
                energy = value * value
                at = (c, pl.ds(t * batch + b, 1))
                sums[at] = jnp.sum(energy, axis=0, keepdims=True)
                moments[at] = jnp.sum(energy * down_k, axis=0, keepdims=True)
        return carry

    lax.fori_loop(0, pairs // batch, turn, 0, unroll=2)

    across = lax.broadcasted_iota(jnp.int32, (pairs, width), 1)
    across = jnp.where(across < length, across, across - width).astype(F32) * 0.5
    live = lax.broadcasted_iota(jnp.int32, (pairs, 1), 0) < count_s[0]
    cells = 1.0 / (width * width)
    shift_all = moves[...]
    spot = lax.broadcasted_iota(jnp.int32, (pairs, partial.shape[1]), 1).astype(F32)
    spread = (spot == shift_all[:, 2 * chips:2 * chips + 1]).astype(F32) - (
        spot == shift_all[:, 2 * chips + 1:2 * chips + 2]
    ).astype(F32)
    columns = [None] * (2 * chips)
    for c in range(chips):
        held = sums[c]
        scale = jnp.sum(held, axis=1, keepdims=True) * cells + 1e-6
        low = jnp.sum(moments[c], axis=1, keepdims=True) * cells
        side = jnp.sum(held * across, axis=1, keepdims=True) * cells
        for x, value in enumerate((low, side)):
            k = x * chips + c
            columns[k] = jnp.where(live, shift_all[:, k:k + 1] + value / scale, 0.0)
    place = lax.broadcasted_iota(jnp.int32, (pairs, width), 1)
    table = jnp.zeros((pairs, width), F32)
    for k, column in enumerate(columns):
        table = jnp.where(place == k, column, table)
        partial[k:k + 1] = jnp.sum(column * spread, axis=0, keepdims=True)
    turned_table = jnp.transpose(table)
    for x in range(2):
        offsets_out[x] = turned_table[x * chips:(x + 1) * chips]

    peers = [lax.rem(me + j, n) for j in range(1, n)]
    copies = []
    for j, peer in enumerate(peers):
        copies.append(
            pltpu.make_async_remote_copy(
                src_ref=partial,
                dst_ref=held_sums.at[j],
                send_sem=send.at[send.shape[0] - n + 1 + j],
                recv_sem=recv.at[recv.shape[0] - n + 1 + j],
                device_id={"date": peer},
                device_id_type=MESH,
            )
        )
        copies[-1].start()
    total = partial[...]
    for j, copy in enumerate(copies):
        copy.wait_recv()
        total = total + held_sums[j]
    total_out[...] = total
    for copy in copies:
        copy.wait_send()


def series_kernel(total, inverse, offsets, series_out, offsets_out):
    offsets_out[...] = offsets[...]
    chips = series_out.shape[1]
    for k in range(inverse.shape[0]):
        value = jnp.sum(inverse[k] * total[k:k + 1], axis=1)[None]
        series_out[k // chips, k % chips:k % chips + 1] = value


def body(n, strips, images, inverse, first, block, second, count, shifts, anchors):
    dates, length, cols = images.shape
    pairs, chips = first.shape[0], anchors.shape[0]
    vmem, smem = pl.BlockSpec(memory_space=pltpu.VMEM), pl.BlockSpec(memory_space=pltpu.SMEM)
    tables = make_tables(length)
    kinds = (30 if n == 8 else 2 * n) + n - 1
    width = 2 * length
    batch = math.gcd(16, math.gcd(pairs, dates))
    offsets, total = pl.pallas_call(
        functools.partial(pairs_kernel, n, strips, batch),
        name="pairs",
        out_shape=(
            jax.ShapeDtypeStruct((2, chips, pairs), F32),
            jax.ShapeDtypeStruct((2 * chips, n * dates), F32),
        ),
        in_specs=[smem] * 6 + [pl.BlockSpec(memory_space=pl.ANY)] * 5,
        out_specs=(vmem, vmem),
        scratch_shapes=[
            *[pltpu.VMEM(table.shape, BF16) for table in tables],
            pltpu.VMEM((n, dates, length, cols), BF16),
            pltpu.VMEM((n, 2, dates, SMAX, cols), BF16),
            pltpu.VMEM((2 * chips, n * dates), F32),
            pltpu.VMEM((n - 1, 2 * chips, n * dates), F32),
            pltpu.SemaphoreType.DMA((1 + len(tables),)),
            pltpu.SemaphoreType.DMA((kinds,)),
            pltpu.SemaphoreType.DMA((kinds,)),
            pltpu.VMEM((pairs, length + 2 * SMAX, cols), F32),
            pltpu.VMEM((pairs * chips, length, cols), BF16),
            pltpu.VMEM((dates * chips, length, cols), BF16),
            pltpu.VMEM((dates * chips, length, 2 * width), BF16),
            pltpu.VMEM((chips, pairs, width), F32),
            pltpu.VMEM((chips, pairs, width), F32),
            pltpu.VMEM((pairs, cols), F32),
        ],
        compiler_params=pltpu.CompilerParams(collective_id=0, has_side_effects=True),
    )(
        first, block.reshape(pairs), second, count, jnp.transpose(shifts, (1, 2, 0)), anchors,
        images, *tables,
    )
    share = inverse.shape[2]
    series, offsets = pl.pallas_call(
        series_kernel,
        name="series",
        out_shape=(
            jax.ShapeDtypeStruct((2, chips, share), F32),
            jax.ShapeDtypeStruct((2, chips, pairs), F32),
        ),
        in_specs=[vmem] * 3,
        out_specs=(vmem, vmem),
    )(total, inverse.reshape(2 * chips, share, n * dates), offsets)
    return jnp.transpose(offsets, (2, 0, 1)), series


def solution(mesh):
    return jax.shard_map(
        functools.partial(body, mesh.shape["date"], mesh.shape["strip"]),
        mesh=mesh,
        in_specs=(
            P("date", "strip", None),
            P(None, "strip", "date", None),
            P("date"),
            P("date", None),
            P("date"),
            P("date"),
            P("date", None, "strip"),
            P("strip"),
        ),
        out_specs=(P("date", None, "strip"), P(None, "strip", "date")),
        check_vma=False,
    )
```
